768 devices in a mesh: dp: 96 (over y, z), group: 8 (over x, core).
Axes of the slice: x: 4, y: 8, z: 12, core: 2. Of those that a mesh axis runs over, the one named last changes fastest.
Arguments:
- queries: bfloat16 [98304, 2048], P(('dp', 'group')), may hold values from -100 to 100
- key_states: bfloat16 [98304, 512], P(('dp', 'group')), may hold values from -4 to 4
- value_states: bfloat16 [98304, 512], P(('dp', 'group')), may hold values from -6 to 6
- grad_out: bfloat16 [98304, 2048], P(('dp', 'group')), may hold values from -6 to 6
- doc_ids: int32 [98304], P(('dp', 'group')), may hold values from 0 to 145, never falling along the last dimension, each value on 1 to 896 neighbouring positions
Outputs:
- attended: bfloat16 [98304, 2048], P(('dp', 'group'))
- grad_queries: bfloat16 [98304, 2048], P(('dp', 'group'))
- grad_keys: bfloat16 [98304, 512], P(('dp', 'group'))
- grad_values: bfloat16 [98304, 512], P(('dp', 'group'))
The draws below stay inside these ranges and needn't reach their ends.
Inputs may be any that keep to these rules, and one draw needn't show every extreme that they name: `doc_ids`: ids never fall along the window; every document holds 1 to 896 tokens, and some document exactly 896.
All inputs are finite; a program needn't handle non-finite values.
Results may differ from the reference program's by a relative error of at most 0.02.
Values may be sent and summed in bfloat16 or wider, within the bound.
A program may use at most 32 MiB of HBM per device.

```python
import math
import jax
import jax.numpy as jnp
import numpy as np
from jax import lax

HEADS = 16
KV_HEADS = 4
HEAD = 128
TOK_DEV = 128
WINDOW = 8
TOKENS = 98304
MAXDOC = 896
NDOCS = 146


def key_field(key):
    base = jax.random.normal(jax.random.fold_in(key, 7), (TOKENS, KV_HEADS * HEAD), jnp.float32)
    return jnp.clip(base, -4.0, 4.0)


def draw_key_states(key, part):
    return key_field(key).astype(jnp.bfloat16)


def draw_queries(key, part):
    drawn = jax.random.normal(jax.random.fold_in(key, 13), (TOKENS, HEADS * HEAD), jnp.float32)
    drawn = jnp.clip(drawn, -4.0, 4.0)
    return drawn.astype(jnp.bfloat16)


def shard_levels(own_key, extent, split, least, largest):
    loudness, own = 1.0, jax.random.fold_in(own_key, 6)
    for dim, parts in split:
        steps = jnp.exp(jax.random.uniform(jax.random.fold_in(own, dim), (parts,), jnp.float32, least / len(split), largest / len(split)))
        loudness = loudness * jnp.repeat(steps, extent[dim] // parts).reshape([-1 if axis == dim else 1 for axis in range(len(extent))])
    return loudness


def split_up(count, total, reach, skew):
    portions = [(1 << 20) // math.isqrt(grade ** skew) + 1 for grade in range(2, count + 1)]
    spare, counts = total - reach - (count - 1), [1] * (count - 1)
    while spare > 0:
        movable = [i for i in range(count - 1) if counts[i] < reach]
        whole, left = sum([portions[i] for i in movable]), spare
        for i in movable:
            addition = min(reach - counts[i], max(1, left * portions[i] // whole), spare)
            counts[i] = counts[i] + addition
            spare = spare - addition
    return np.array([reach] + counts)


def uneven(rng, amount, total, bound, skew):
    if amount == 2:
        one = jax.random.randint(rng, (), max(1, total - bound), min(bound, total - 1) + 1)
        return jnp.stack([one, total - one])
    sizes = jnp.asarray(split_up(amount, total, bound, skew), jnp.int32)
    pairs = (amount - 1) // 2
    giver, taker = sizes[1:1 + 2 * pairs:2], sizes[2:2 + 2 * pairs:2]
    room = jnp.minimum(giver - 1, bound - taker)
    passed = jax.random.randint(jax.random.fold_in(rng, 1), (pairs,), 0, 1 << 20) % (room + 1)
    sizes = sizes.at[1:1 + 2 * pairs:2].set(giver - passed).at[2:2 + 2 * pairs:2].set(taker + passed)
    return sizes[jax.random.permutation(jax.random.fold_in(rng, 2), amount)]


def scatter_about(rng, dims, scale, reach, shards=(), held_as=jnp.bfloat16):
    drawn = scale * jax.random.normal(rng, dims, jnp.float32)
    if shards:
        drawn = drawn * shard_levels(rng, dims, shards, -0.22, 0.18)
    return jnp.clip(drawn, -reach, reach).astype(held_as)


def setup_inputs(seed: int = 0) -> dict:
    arg_keys = jax.random.split(jax.random.key(seed), 6)
    return {
        "queries": draw_queries(jax.random.fold_in(arg_keys[5], 71), 0),
        "key_states": draw_key_states(jax.random.fold_in(arg_keys[5], 71), 0),
        "value_states": scatter_about(arg_keys[2], (TOKENS, KV_HEADS * HEAD), 1.0, 6.0, ((0, 768),)),
        "grad_out": scatter_about(arg_keys[3], (TOKENS, HEADS * HEAD), 1.0, 6.0, ((0, 768),)),
        "doc_ids": jnp.searchsorted(jnp.cumsum(uneven(arg_keys[4], NDOCS, TOKENS, MAXDOC, 0)), jnp.arange(TOKENS), side="right").astype(jnp.int32),
    }


def attend(query_head, key_head, value_head, grad_head, allowed):
    softmax_scale = HEAD ** -0.5
    query_full = query_head.astype(jnp.float32)
    key_full = key_head.astype(jnp.float32)
    value_full = value_head.astype(jnp.float32)
    grad_full = grad_head.astype(jnp.float32)
    scores = jnp.einsum("igd,jd->gij", query_full, key_full) * softmax_scale
    scores = jnp.where(allowed[None], scores, -jnp.inf)
    row_max = jnp.max(scores, axis=-1, keepdims=True)
    log_total = row_max + jnp.log(jnp.sum(jnp.exp(scores - row_max), axis=-1, keepdims=True))
    weights = jnp.where(allowed[None], jnp.exp(scores - log_total), 0.0)
    probs_low = weights.astype(jnp.bfloat16)
    output = jnp.einsum("gij,jd->igd", probs_low.astype(jnp.float32), value_full).astype(jnp.bfloat16)
    row_delta = jnp.sum(grad_full * output.astype(jnp.float32), axis=-1)
    grad_probs = jnp.einsum("igd,jd->gij", grad_full, value_full)
    grad_scores = (weights * (grad_probs - row_delta.T[:, :, None]) * softmax_scale).astype(jnp.bfloat16)
    grad_scores_full = grad_scores.astype(jnp.float32)
    grad_query = jnp.einsum("gij,jd->igd", grad_scores_full, key_full).astype(jnp.bfloat16)
    grad_key = jnp.einsum("gij,igd->jd", grad_scores_full, query_full)
    grad_value = jnp.einsum("gij,igd->jd", probs_low.astype(jnp.float32), grad_full)
    return output, grad_query, grad_key, grad_value


def reference(queries, key_states, value_states, grad_out, doc_ids):
    blocks = TOKENS // TOK_DEV
    margin = (WINDOW - 1) * TOK_DEV
    window_len = WINDOW * TOK_DEV
    groups = HEADS // KV_HEADS
    key_padded = jnp.concatenate([jnp.zeros((margin, KV_HEADS * HEAD), key_states.dtype), key_states], 0)
    value_padded = jnp.concatenate([jnp.zeros((margin, KV_HEADS * HEAD), value_states.dtype), value_states], 0)
    ids_padded = jnp.concatenate([jnp.full((margin,), -1, jnp.int32), doc_ids.astype(jnp.int32)], 0)
    query_index = jnp.arange(TOK_DEV, dtype=jnp.int32)
    window_index = jnp.arange(window_len, dtype=jnp.int32)
    vmapped = jax.vmap(attend, in_axes=(1, 1, 1, 1, None), out_axes=(1, 1, 1, 1))

    def one_block(totals, block_id):
        grad_keys, grad_values = totals
        first_row = (block_id * TOK_DEV).astype(jnp.int32)
        query_rows = lax.dynamic_slice_in_dim(queries, first_row, TOK_DEV, 0).reshape(TOK_DEV, KV_HEADS, groups, HEAD)
        grad_rows = lax.dynamic_slice_in_dim(grad_out, first_row, TOK_DEV, 0).reshape(TOK_DEV, KV_HEADS, groups, HEAD)
        query_ids = lax.dynamic_slice_in_dim(doc_ids.astype(jnp.int32), first_row, TOK_DEV, 0)
        key_rows = lax.dynamic_slice_in_dim(key_padded, first_row, window_len, 0).reshape(window_len, KV_HEADS, HEAD)
        value_rows = lax.dynamic_slice_in_dim(value_padded, first_row, window_len, 0).reshape(window_len, KV_HEADS, HEAD)
        key_ids = lax.dynamic_slice_in_dim(ids_padded, first_row, window_len, 0)
        allowed = (key_ids[None, :] == query_ids[:, None]) & (window_index[None, :] - margin <= query_index[:, None])
        output, grad_query, grad_key, grad_value = vmapped(query_rows, key_rows, value_rows, grad_rows, allowed)
        old_keys = lax.dynamic_slice_in_dim(grad_keys, first_row, window_len, 0)
        grad_keys = lax.dynamic_update_slice_in_dim(grad_keys, old_keys + grad_key.reshape(window_len, KV_HEADS * HEAD), first_row, 0)
        old_values = lax.dynamic_slice_in_dim(grad_values, first_row, window_len, 0)
        grad_values = lax.dynamic_update_slice_in_dim(grad_values, old_values + grad_value.reshape(window_len, KV_HEADS * HEAD), first_row, 0)
        return (grad_keys, grad_values), (output.reshape(TOK_DEV, HEADS * HEAD), grad_query.reshape(TOK_DEV, HEADS * HEAD))

    zero_field = jnp.zeros((TOKENS + margin, KV_HEADS * HEAD), jnp.float32)
    (grad_keys, grad_values), (outputs, grad_queries) = lax.scan(one_block, (zero_field, zero_field), jnp.arange(blocks, dtype=jnp.int32))
    return (outputs.reshape(TOKENS, HEADS * HEAD), grad_queries.reshape(TOKENS, HEADS * HEAD), grad_keys[margin:].astype(jnp.bfloat16), grad_values[margin:].astype(jnp.bfloat16))
```

```python
import functools

import jax
import jax.numpy as jnp
from jax import lax
from jax.experimental import pallas as pl
from jax.experimental.pallas import tpu as pltpu
from jax.sharding import PartitionSpec as P

MESH = pl.DeviceIdType.MESH
BF16, F32 = jnp.bfloat16, jnp.float32
SCALE = 128 ** -0.5
LOG2E = 1.4426950408889634
BIG = -1e30


def nt(a, b):
    return lax.dot_general(a, b, (((1,), (1,)), ((), ())), preferred_element_type=F32)


def nn(a, b):
    return lax.dot_general(a, b, (((1,), (0,)), ((), ())), preferred_element_type=F32)


def tn(a, b):
    return lax.dot_general(a, b, (((0,), (0,)), ((), ())), preferred_element_type=F32)


def kernel(
    rows_dp, q_in, k_in, v_in, g_in, ids_in, o_out, dq_out, dk_out, dv_out,
    Q, G, K, V, IDS, BIAS, PF, PR, DS, OB, ACC, SND, RCV, OWN, SIB, FIN,
    own_sem, gs_sem, gr_sem, ql_sem, qs_sem, qr_sem,
    rs_sem, rr_sem, ol_sem, os_sem, or_sem, fl_sem, fs_sem, fr_sem,
):
    dp, group = lax.axis_index("dp"), lax.axis_index("group")
    x, k = group // 2, group % 2
    odd = x % 2
    last, first = x // 3, (3 - x) // 3
    nxt, prv = (dp + 1) % rows_dp, (dp + rows_dp - 1) % rows_dp
    sib = (dp, x * 2 + 1 - k)

    def along(step):
        return (dp, ((x + step) % 4) * 2 + k)

    z_next, z_prev = (nxt, group), (prv, group)
    partner_k = (dp, ((x + 1 + 2 * odd) % 4) * 2 + k)
    partner_v = ((dp + last + rows_dp - first) % rows_dp, ((x + 3 + 2 * odd) % 4) * 2 + k)
    relay_k, relay_v = 3 - 2 * odd, 1 + 2 * odd

    def spot(m, pos, core):
        if m == 0:
            return IDS.at[pos, core]
        buf = K if m % 2 else V
        return buf.at[(m - 1) // 2, pl.ds(pl.multiple_of(pos * 256 + core * 128, 128), 128), :]

    def source(m, core):
        if m == 0:
            return ids_in
        arr = k_in if m % 2 else v_in
        return arr.at[:, pl.ds(pl.multiple_of((2 * core + (m - 1) // 2) * 128, 128), 128)]

    def remote(src, dst, send, recv, dev):
        return pltpu.make_async_remote_copy(
            src_ref=src, dst_ref=dst, send_sem=send, recv_sem=recv, device_id=dev, device_id_type=MESH
        )

    def own_copy(m):
        return pltpu.make_async_copy(source(m, k), spot(m, 4, k), own_sem.at[m])

    def sib_send(m):
        return remote(source(m, 1 - k), spot(m, 4, k), gs_sem.at[m, 4, 0], gr_sem.at[m, 4, 0], sib)

    def sib_wait(m):
        remote(source(m, k), spot(m, 4, 1 - k), gs_sem.at[m, 4, 0], gr_sem.at[m, 4, 0], sib).wait_recv()

    def send_own(m, pos, dev):
        for n, core in enumerate((k, 1 - k)):
            target = (dev[0], dev[1] - k + core)
            remote(source(m, core), spot(m, pos, k), gs_sem.at[m, pos, n], gr_sem.at[m, pos, k], target).start()

    def edge(m, src_pos, pos, dev, part):
        return remote(
            spot(m, src_pos, part), spot(m, pos, part), gs_sem.at[m, pos, part], gr_sem.at[m, pos, part], dev
        )

    def arrived(m, pos):
        for part in range(2):
            edge(m, pos, pos, sib, part).wait_recv()

    msgs = range(5)
    for m in msgs:
        own_copy(m).start()
    half_q = pl.ds(pl.multiple_of(k * 1024, 1024), 1024)
    half_s = pl.ds(pl.multiple_of((1 - k) * 1024, 1024), 1024)
    q_own = [
        pltpu.make_async_copy(arr.at[:, half_q], buf.at[k], ql_sem.at[i])
        for i, (arr, buf) in enumerate(((q_in, Q), (g_in, G)))
    ]
    q_send = [
        remote(arr.at[:, half_s], buf.at[k], qs_sem.at[i], qr_sem.at[i], sib)
        for i, (arr, buf) in enumerate(((q_in, Q), (g_in, G)))
    ]
    q_recv = [
        remote(arr.at[:, half_q], buf.at[1 - k], qs_sem.at[i], qr_sem.at[i], sib)
        for i, (arr, buf) in enumerate(((q_in, Q), (g_in, G)))
    ]
    for copy in q_own:
        copy.start()

    barrier = pltpu.get_barrier_semaphore()
    for dev in (sib, along(1), along(2), along(3), z_next, z_prev, partner_v):
        pl.semaphore_signal(barrier, inc=1, device_id=dev, device_id_type=MESH)
    for dev in (along(1), along(3), z_next, z_prev):
        other = (dev[0], dev[1] + 1 - 2 * k)
        pl.semaphore_signal(barrier, inc=1, device_id=other, device_id_type=MESH)
    pl.semaphore_wait(barrier, 11)

    for m in msgs:
        send_own(m, 0, z_next)
        sib_send(m).start()

        @pl.when(x < 3)
        def _():
            send_own(m, 3, along(1))

        @pl.when(x == 0)
        def _():
            send_own(m, 1, along(3))

    for copy in q_send:
        copy.start()

    def forward(m):
        for part in range(2):
            edge(m, 0, 0, sib, part).wait_recv()

            @pl.when(x == 3)
            def _():
                edge(m, 0, 3, along(1), part).start()

            @pl.when(x > 0)
            def _():
                edge(m, 0, 1, along(3), part).start()

    def relay_pos(m):
        return relay_k if m % 2 or m == 0 else relay_v

    def relay(m):
        for part in range(2):
            edge(m, relay_pos(m), relay_pos(m), sib, part).wait_recv()
            edge(m, relay_pos(m), 2, partner_k if m % 2 or m == 0 else partner_v, part).start()

    def complete(m):
        own_copy(m).wait()
        sib_wait(m)
        arrived(m, 4 - relay_pos(m))
        arrived(m, 2)

    for m in (0, 1, 2):
        forward(m)
    relay(0)
    forward(3)
    relay(1)
    forward(4)
    relay(2)
    complete(0)

    chip = 4 * dp + x
    col = lax.broadcasted_iota(jnp.int32, (128, 1024), 1)
    row = lax.broadcasted_iota(jnp.int32, (128, 1024), 0)
    ids = [IDS[b // 2, b % 2] for b in range(10)]
    for t in range(2):
        key_ids = jnp.broadcast_to(jnp.concatenate(ids[1 + t : 9 + t], 1), (128, 1024))
        own_ids = jnp.transpose(jnp.broadcast_to(ids[8 + t], (128, 128)))
        query_ids = jnp.concatenate([own_ids] * 8, 1)
        allowed = (key_ids == query_ids) & (col <= row + 896) & (col >= 128 * (7 - t - 2 * chip))
        BIAS[t] = jnp.where(allowed, 0.0, BIG)
    for copy in q_own:
        copy.wait()
    for copy in q_recv:
        copy.wait_recv()

    def heads_of(ref, t, h):
        return jnp.concatenate([ref[t, :, (4 * h + i) * 128 : (4 * h + i + 1) * 128] for i in range(4)], 0)

    def weigh(h, t):
        lo = 128 * (1 + t)
        scores = nt(heads_of(Q, t, h), K[h, lo : lo + 1024, :]) * (SCALE * LOG2E)
        scores = scores + jnp.concatenate([BIAS[t]] * 4, 0)
        exps = jnp.exp2(scores - jnp.max(scores, -1, keepdims=True))
        probs = exps * (1.0 / jnp.sum(exps, -1, keepdims=True))
        PF[t] = probs
        PR[t, :, lo : lo + 1024] = probs.astype(BF16)

    def attend(h, t):
        lo = 128 * (1 + t)
        keys, values = K[h, lo : lo + 1024, :], V[h, lo : lo + 1024, :]
        g = heads_of(G, t, h)
        out = nn(PR[t, :, lo : lo + 1024], values).astype(BF16)
        delta = jnp.sum(g.astype(F32) * out.astype(F32), -1, keepdims=True)
        grads = (PF[t] * (nt(g, values) - delta)).astype(BF16)
        DS[t, :, lo : lo + 1024] = grads
        dq = (nn(grads, keys) * SCALE).astype(BF16)
        for i in range(4):
            OB[0, h, t, :, i * 128 : (i + 1) * 128] = out[i * 128 : (i + 1) * 128]
            OB[1, h, t, :, i * 128 : (i + 1) * 128] = dq[i * 128 : (i + 1) * 128]
        for n, arr in enumerate((o_out, dq_out)):

            @pl.when(k == t)
            def _():
                out_local(n, arr, h, t).start()

            @pl.when(k != t)
            def _():
                out_remote(n, arr, h, t, k).start()

    def wide(h, core):
        return pl.ds(pl.multiple_of((2 * core + h) * 512, 512), 512)

    def out_local(n, arr, h, t):
        return pltpu.make_async_copy(OB.at[n, h, t], arr.at[:, wide(h, k)], ol_sem.at[n, h])

    def out_remote(n, arr, h, t, core):
        return remote(OB.at[n, h, t], arr.at[:, wide(h, core)], os_sem.at[n, h], or_sem.at[n, h], sib)

    def send_part(n, pos, part, dev):
        return remote(
            SND.at[n, pos, part], RCV.at[n, pos, part], rs_sem.at[n, pos, part], rr_sem.at[n, pos, part], dev
        )

    def send_back(n, part, core):
        dev = (prv, x * 2 + part)
        return remote(SND.at[n, 0, part], RCV.at[n, 0, core], rs_sem.at[n, 0, part], rr_sem.at[n, 0, core], dev)

    def send_sib(n):
        return remote(SIB.at[n, 0], SIB.at[n, 1], fs_sem.at[n], fr_sem.at[n], sib)

    def part_wait(n, pos, part):
        send_part(n, pos, part, sib).wait_recv()

    def fold_pos(n):
        return relay_k if n % 2 else relay_v

    def ship(n, pos, dev):
        for part in range(2):
            SND[n, pos, part] = ACC[n, pos, :, part * 128 : (part + 1) * 128].astype(BF16)
            send_part(n, pos, part, dev).start()

    def partials(n):
        h = n // 2
        left, right, scale = (Q, DS, SCALE) if n % 2 else (G, PR, 1.0)
        a0, a1 = heads_of(left, 0, h), heads_of(left, 1, h)

        def term(t, lo, hi):
            return tn(a1 if t else a0, right[t, :, lo:hi]) * scale

        for pos in (2, 1, 3):
            ACC[n, pos] = term(0, pos * 256, pos * 256 + 256) + term(1, pos * 256, pos * 256 + 256)
            if pos == 2:
                ship(n, 2, along(2) if n == 3 else (partner_k if n % 2 else partner_v))
            elif n == 3:
                ship(n, pos, along(pos))
        if n < 3:
            ship(n, 4 - fold_pos(n), along(4 - fold_pos(n)))
        ACC[n, 0, :, :128] = jnp.zeros((128, 128), F32)
        ACC[n, 0, :, 128:] = term(0, 128, 256)
        ACC[n, 4, :, :128] = term(0, 1024, 1152) + term(1, 1024, 1152)
        ACC[n, 4, :, 128:] = term(1, 1152, 1280)

    def fold(n):
        pos = fold_pos(n)
        for part in range(2):
            part_wait(n, 2, part)
            total = ACC[n, pos, :, part * 128 : (part + 1) * 128] + RCV[n, 2, part].astype(F32)
            SND[n, pos, part] = total.astype(BF16)
            send_part(n, pos, part, along(pos)).start()

    def split(n):
        for part in range(2):
            cols = slice(part * 128, (part + 1) * 128)
            part_wait(n, 1, part)
            part_wait(n, 3, part)
            ahead, behind = RCV[n, 3, part].astype(F32), RCV[n, 1, part].astype(F32)
            zero = jnp.zeros_like(ahead)
            to_prev = ACC[n, 0, :, cols] + jnp.where(x == 3, ahead, zero) + jnp.where(x > 0, behind, zero)
            mine = ACC[n, 4, :, cols] + jnp.where(x < 3, ahead, zero) + jnp.where(x == 0, behind, zero)
            if n == 3:
                part_wait(n, 2, part)
                across = RCV[n, 2, part].astype(F32)
                to_prev = to_prev + jnp.where(x >= 2, across, zero)
                mine = mine + jnp.where(x < 2, across, zero)
            SND[n, 0, part] = to_prev.astype(BF16)
            send_back(n, part, k).start()
            OWN[n, part] = mine
        SIB[n, 0] = OWN[n, 1 - k].astype(BF16)
        send_sib(n).start()

    def narrow(n, core):
        return pl.ds(pl.multiple_of((2 * core + n // 2) * 128, 128), 128)

    def fin_local(n, side):
        core = 1 - k if side else k
        return pltpu.make_async_copy(
            FIN.at[n, side], (dk_out if n % 2 else dv_out).at[:, narrow(n, core)], fl_sem.at[n, side]
        )

    def finish(n):
        remote(SND.at[n, 0, 0], RCV.at[n, 0, k], rs_sem.at[n, 0, 0], rr_sem.at[n, 0, k], sib).wait_recv()
        FIN[n, 0] = jnp.transpose(OWN[n, k] + RCV[n, 0, k].astype(F32)).astype(BF16)
        fin_local(n, 0).start()
        remote(SND.at[n, 0, 0], RCV.at[n, 0, 1 - k], rs_sem.at[n, 0, 0], rr_sem.at[n, 0, 1 - k], sib).wait_recv()
        send_sib(n).wait_recv()
        FIN[n, 1] = jnp.transpose(SIB[n, 1].astype(F32) + RCV[n, 0, 1 - k].astype(F32)).astype(BF16)
        fin_local(n, 1).start()

    complete(1)
    weigh(0, 0)
    relay(3)
    weigh(0, 1)
    partials(0)
    relay(4)
    complete(2)
    attend(0, 0)
    attend(0, 1)
    partials(1)
    complete(3)
    weigh(1, 0)
    fold(0)
    weigh(1, 1)
    partials(2)
    complete(4)
    fold(1)
    attend(1, 0)
    split(0)
    attend(1, 1)
    fold(2)
    partials(3)
    split(1)
    finish(0)
    split(2)
    finish(1)
    split(3)
    finish(2)
    finish(3)

    for n in range(4):
        send_sib(n).wait_send()
        for part in range(2):
            fin_local(n, part).wait()
            for pos in range(4):
                send_part(n, pos, part, sib).wait_send()
    for n, arr in enumerate((o_out, dq_out)):
        for h in range(2):
            out_local(n, arr, h, k).wait()
            out_remote(n, arr, h, 1 - k, k).wait_send()
            out_remote(n, arr, h, 1 - k, 1 - k).wait_recv()
    for copy in q_send:
        copy.wait_send()
    for m in msgs:
        sib_send(m).wait_send()
        for pos in range(4):
            for part in range(2):
                edge(m, pos, pos, sib, part).wait_send()


def put_out(*refs):
    copies = [pltpu.make_async_copy(refs[i], refs[4 + i], refs[8].at[i]) for i in range(4)]
    for copy in copies:
        copy.start()
    for copy in copies:
        copy.wait()


def solution(mesh):
    rows_dp = mesh.shape["dp"]

    def local(queries, key_states, value_states, grad_out, doc_ids):
        hbm, place = pl.BlockSpec(memory_space=pltpu.HBM), pl.BlockSpec(memory_space=pl.ANY)
        dma, vmem = pltpu.SemaphoreType.DMA, pltpu.VMEM
        shapes = tuple(jax.ShapeDtypeStruct((128, width), BF16) for width in (2048, 2048, 512, 512))
        made = pl.pallas_call(
            functools.partial(kernel, rows_dp),
            out_shape=shapes,
            in_specs=[hbm] * 5,
            out_specs=(place,) * 4,
            scratch_shapes=[
                vmem((2, 128, 1024), BF16),
                vmem((2, 128, 1024), BF16),
                vmem((2, 1280, 128), BF16),
                vmem((2, 1280, 128), BF16),
                vmem((5, 2, 1, 128), jnp.int32),
                vmem((2, 128, 1024), F32),
                vmem((2, 512, 1024), F32),
                vmem((2, 512, 1280), BF16),
                vmem((2, 512, 1280), BF16),
                vmem((2, 2, 2, 128, 512), BF16),
                vmem((4, 5, 128, 256), F32),
                vmem((4, 4, 2, 128, 128), BF16),
                vmem((4, 4, 2, 128, 128), BF16),
                vmem((4, 2, 128, 128), F32),
                vmem((4, 2, 128, 128), BF16),
                vmem((4, 2, 128, 128), BF16),
                dma((5,)),
                dma((5, 5, 2)),
                dma((5, 5, 2)),
                dma((2,)),
                dma((2,)),
                dma((2,)),
                dma((4, 4, 2)),
                dma((4, 4, 2)),
                dma((2, 2)),
                dma((2, 2)),
                dma((2, 2)),
                dma((4, 2)),
                dma((4,)),
                dma((4,)),
            ],
            compiler_params=pltpu.CompilerParams(
                collective_id=0, has_side_effects=True, vmem_limit_bytes=48 * 1024 * 1024
            ),
        )(*[pltpu.with_memory_space_constraint(z, pltpu.HBM) for z in (queries, key_states, value_states, grad_out, doc_ids.reshape(1, 128))])
        return pl.pallas_call(
            put_out,
            out_shape=shapes,
            in_specs=[place] * 4,
            out_specs=(hbm,) * 4,
            scratch_shapes=[dma((4,))],
            compiler_params=pltpu.CompilerParams(vmem_limit_bytes=1024 * 1024),
        )(*made)

    row, flat = P(("dp", "group"), None), P(("dp", "group"))
    return jax.shard_map(
        local,
        mesh=mesh,
        in_specs=(row, row, row, row, flat),
        out_specs=(row,) * 4,
        check_vma=False,
    )
```

```python
import functools

import jax
import jax.numpy as jnp
from jax import lax
from jax.experimental import pallas as pl
from jax.experimental.pallas import tpu as pltpu
from jax.sharding import PartitionSpec as P

MESH = pl.DeviceIdType.MESH
BF16, F32 = jnp.bfloat16, jnp.float32
SCALE = 128 ** -0.5
LOG2E = 1.4426950408889634
BIG = -1e30


def nt(a, b):
    return lax.dot_general(a, b, (((1,), (1,)), ((), ())), preferred_element_type=F32)


def nn(a, b):
    return lax.dot_general(a, b, (((1,), (0,)), ((), ())), preferred_element_type=F32)


def tn(a, b):
    return lax.dot_general(a, b, (((0,), (0,)), ((), ())), preferred_element_type=F32)


def kernel(
    rows_dp, q_in, k_in, v_in, g_in, ids_in, o_out, dq_out, dk_out, dv_out,
    Q, G, K, V, IDS, BIAS, PF, PR, DS, OB, ACC, SND, RCV, OWN, SIB, FIN,
    own_sem, gs_sem, gr_sem, ql_sem, qs_sem, qr_sem,
    rs_sem, rr_sem, ol_sem, os_sem, or_sem, fl_sem, fs_sem, fr_sem,
):
    dp, group = lax.axis_index("dp"), lax.axis_index("group")
    x, k = group // 2, group % 2
    odd = x % 2
    last, first = x // 3, (3 - x) // 3
    nxt, prv = (dp + 1) % rows_dp, (dp + rows_dp - 1) % rows_dp
    sib = (dp, x * 2 + 1 - k)

    def along(step):
        return (dp, ((x + step) % 4) * 2 + k)

    z_next, z_prev = (nxt, group), (prv, group)
    partner = (
        (dp, ((x + 1 + 2 * odd) % 4) * 2 + k),
        ((dp + last + rows_dp - first) % rows_dp, ((x + 3 + 2 * odd) % 4) * 2 + k),
    )
    relay_pos = (3 - 2 * odd, 1 + 2 * odd)

    def spot(m, pos, core):
        if m == 0:
            return IDS.at[pos, core]
        buf = K if m % 2 else V
        return buf.at[(m - 1) // 2, pl.ds(pl.multiple_of(pos * 256 + core * 128, 128), 128), :]

    def source(m, core):
        if m == 0:
            return ids_in
        arr = k_in if m % 2 else v_in
        return arr.at[:, pl.ds(pl.multiple_of((2 * core + (m - 1) // 2) * 128, 128), 128)]

    def remote(src, dst, send, recv, dev):
        return pltpu.make_async_remote_copy(
            src_ref=src, dst_ref=dst, send_sem=send, recv_sem=recv, device_id=dev, device_id_type=MESH
        )

    def own_copy(m):
        return pltpu.make_async_copy(source(m, k), spot(m, 4, k), own_sem.at[m])

    def sib_send(m):
        return remote(source(m, 1 - k), spot(m, 4, k), gs_sem.at[m, 4, 0], gr_sem.at[m, 4, 0], sib)

    def sib_wait(m):
        remote(source(m, k), spot(m, 4, 1 - k), gs_sem.at[m, 4, 0], gr_sem.at[m, 4, 0], sib).wait_recv()

    def send_own(m, pos, dev):
        for n, core in enumerate((k, 1 - k)):
            target = (dev[0], dev[1] - k + core)
            remote(source(m, core), spot(m, pos, k), gs_sem.at[m, pos, n], gr_sem.at[m, pos, k], target).start()

    def edge(m, src_pos, pos, dev, part):
        return remote(
            spot(m, src_pos, part), spot(m, pos, part), gs_sem.at[m, pos, part], gr_sem.at[m, pos, part], dev
        )

    def arrived(m, pos):
        for part in range(2):
            edge(m, pos, pos, sib, part).wait_recv()

    barrier = pltpu.get_barrier_semaphore()
    for dev in (sib, along(1), along(2), along(3), z_next, z_prev, partner[1]):
        pl.semaphore_signal(barrier, inc=1, device_id=dev, device_id_type=MESH)
    for dev in (along(1), along(3), z_next, z_prev):
        other = (dev[0], dev[1] + 1 - 2 * k)
        pl.semaphore_signal(barrier, inc=1, device_id=other, device_id_type=MESH)
    msgs = range(5)
    for m in msgs:
        own_copy(m).start()
    half_q = pl.ds(pl.multiple_of(k * 1024, 1024), 1024)
    half_s = pl.ds(pl.multiple_of((1 - k) * 1024, 1024), 1024)
    q_own = [
        pltpu.make_async_copy(arr.at[:, half_q], buf.at[k], ql_sem.at[i])
        for i, (arr, buf) in enumerate(((q_in, Q), (g_in, G)))
    ]
    q_send = [
        remote(arr.at[:, half_s], buf.at[k], qs_sem.at[i], qr_sem.at[i], sib)
        for i, (arr, buf) in enumerate(((q_in, Q), (g_in, G)))
    ]
    q_recv = [
        remote(arr.at[:, half_q], buf.at[1 - k], qs_sem.at[i], qr_sem.at[i], sib)
        for i, (arr, buf) in enumerate(((q_in, Q), (g_in, G)))
    ]
    for copy in q_own:
        copy.start()

    pl.semaphore_wait(barrier, 11)

    for m in msgs:
        send_own(m, 0, z_next)
    for m in msgs:
        sib_send(m).start()

        @pl.when(x < 3)
        def _():
            send_own(m, 3, along(1))

        @pl.when(x == 0)
        def _():
            send_own(m, 1, along(3))

    for copy in q_send:
        copy.start()

    def forward(m):
        for part in range(2):
            edge(m, 0, 0, sib, part).wait_recv()

            @pl.when(x == 3)
            def _():
                edge(m, 0, 3, along(1), part).start()

            @pl.when(x > 0)
            def _():
                edge(m, 0, 1, along(3), part).start()

    def relay(m):
        for part in range(2):
            pos = relay_pos[part]
            edge(m, pos, pos, sib, part).wait_recv()
            edge(m, pos, 2, partner[part], part).start()

    def complete(m):
        own_copy(m).wait()
        sib_wait(m)
        for part in range(2):
            edge(m, 4 - relay_pos[part], 4 - relay_pos[part], sib, part).wait_recv()
            edge(m, 2, 2, sib, part).wait_recv()

    for m in (0, 1, 2):
        forward(m)
    relay(0)
    forward(3)
    relay(1)
    forward(4)
    relay(2)
    complete(0)

    chip = 4 * dp + x
    col = lax.broadcasted_iota(jnp.int32, (128, 1024), 1)
    row = lax.broadcasted_iota(jnp.int32, (128, 1024), 0)
    ids = [IDS[b // 2, b % 2] for b in range(10)]
    for t in range(2):
        key_ids = jnp.broadcast_to(jnp.concatenate(ids[1 + t : 9 + t], 1), (128, 1024))
        own_ids = jnp.transpose(jnp.broadcast_to(ids[8 + t], (128, 128)))
        query_ids = jnp.concatenate([own_ids] * 8, 1)
        allowed = (key_ids == query_ids) & (col <= row + 896) & (col >= 128 * (7 - t - 2 * chip))
        BIAS[t] = jnp.where(allowed, 0.0, BIG)
    for copy in q_own:
        copy.wait()
    for copy in q_recv:
        copy.wait_recv()

    def heads_of(ref, t, h):
        return jnp.concatenate([ref[t, :, (4 * h + i) * 128 : (4 * h + i + 1) * 128] for i in range(4)], 0)

    def weigh(h, t):
        lo = 128 * (1 + t)
        scores = nt(heads_of(Q, t, h), K[h, lo : lo + 1024, :]) * (SCALE * LOG2E)
        scores = scores + jnp.concatenate([BIAS[t]] * 4, 0)
        exps = jnp.exp2(scores - jnp.max(scores, -1, keepdims=True))
        probs = exps * (1.0 / jnp.sum(exps, -1, keepdims=True))
        PF[t] = probs
        PR[t, :, lo : lo + 1024] = probs.astype(BF16)

    def put(n, h, t, value):
        for i in range(4):
            OB[n, h, t, :, i * 128 : (i + 1) * 128] = value[i * 128 : (i + 1) * 128]
        arr = (o_out, dq_out)[n]

        @pl.when(k == t)
        def _():
            out_local(n, arr, h, t).start()

        @pl.when(k != t)
        def _():
            out_remote(n, arr, h, t, k).start()

    def attend(h, t):
        lo = 128 * (1 + t)
        values = V[h, lo : lo + 1024, :]
        g = heads_of(G, t, h)
        out = nn(PR[t, :, lo : lo + 1024], values).astype(BF16)
        delta = jnp.sum(g.astype(F32) * out.astype(F32), -1, keepdims=True)
        DS[t, :, lo : lo + 1024] = (PF[t] * (nt(g, values) - delta)).astype(BF16)
        put(0, h, t, out)

    def query_grads(h, t):
        lo = 128 * (1 + t)
        put(1, h, t, (nn(DS[t, :, lo : lo + 1024], K[h, lo : lo + 1024, :]) * SCALE).astype(BF16))

    def wide(h, core):
        return pl.ds(pl.multiple_of((2 * core + h) * 512, 512), 512)

    def out_local(n, arr, h, t):
        return pltpu.make_async_copy(OB.at[n, h, t], arr.at[:, wide(h, k)], ol_sem.at[n, h])

    def out_remote(n, arr, h, t, core):
        return remote(OB.at[n, h, t], arr.at[:, wide(h, core)], os_sem.at[n, h], or_sem.at[n, h], sib)

    def send_part(n, pos, part, dev):
        return remote(
            SND.at[n, pos, part], RCV.at[n, pos, part], rs_sem.at[n, pos, part], rr_sem.at[n, pos, part], dev
        )

    def send_back(n, part, core):
        dev = (prv, x * 2 + part)
        return remote(SND.at[n, 0, part], RCV.at[n, 0, core], rs_sem.at[n, 0, part], rr_sem.at[n, 0, core], dev)

    def send_sib(n):
        return remote(SIB.at[n, 0], SIB.at[n, 1], fs_sem.at[n], fr_sem.at[n], sib)

    def part_wait(n, pos, part):
        send_part(n, pos, part, sib).wait_recv()

    def ship(n, pos, part, dev):
        SND[n, pos, part] = ACC[n, pos, :, part * 128 : (part + 1) * 128].astype(BF16)
        send_part(n, pos, part, dev).start()

    def partials(n):
        h = n // 2
        left, right, scale = (Q, DS, SCALE) if n % 2 else (G, PR, 1.0)
        a0, a1 = heads_of(left, 0, h), heads_of(left, 1, h)

        def term(t, lo, hi):
            return tn(a1 if t else a0, right[t, :, lo:hi]) * scale

        for pos in (2, 1, 3):
            ACC[n, pos] = term(0, pos * 256, pos * 256 + 256) + term(1, pos * 256, pos * 256 + 256)
            for part in range(2):
                if pos == 2:
                    ship(n, 2, part, along(2) if n == 3 else partner[part])
                elif n == 3:
                    ship(n, pos, part, along(pos))
        if n < 3:
            for part in range(2):
                ship(n, 4 - relay_pos[part], part, along(4 - relay_pos[part]))
        ACC[n, 0, :, :128] = jnp.zeros((128, 128), F32)
        ACC[n, 0, :, 128:] = term(0, 128, 256)
        ACC[n, 4, :, :128] = term(0, 1024, 1152) + term(1, 1024, 1152)
        ACC[n, 4, :, 128:] = term(1, 1152, 1280)

    def fold(n):
        for part in range(2):
            pos = relay_pos[part]
            part_wait(n, 2, part)
            total = ACC[n, pos, :, part * 128 : (part + 1) * 128] + RCV[n, 2, part].astype(F32)
            SND[n, pos, part] = total.astype(BF16)
            send_part(n, pos, part, along(pos)).start()

    def split(n):
        for part in range(2):
            cols = slice(part * 128, (part + 1) * 128)
            part_wait(n, 1, part)
            part_wait(n, 3, part)
            ahead, behind = RCV[n, 3, part].astype(F32), RCV[n, 1, part].astype(F32)
            zero = jnp.zeros_like(ahead)
            to_prev = ACC[n, 0, :, cols] + jnp.where(x == 3, ahead, zero) + jnp.where(x > 0, behind, zero)
            mine = ACC[n, 4, :, cols] + jnp.where(x < 3, ahead, zero) + jnp.where(x == 0, behind, zero)
            if n == 3:
                part_wait(n, 2, part)
                across = RCV[n, 2, part].astype(F32)
                to_prev = to_prev + jnp.where(x >= 2, across, zero)
                mine = mine + jnp.where(x < 2, across, zero)
            SND[n, 0, part] = to_prev.astype(BF16)
            send_back(n, part, k).start()
            OWN[n, part] = mine
        SIB[n, 0] = OWN[n, 1 - k].astype(BF16)
        send_sib(n).start()

    def narrow(n, core):
        return pl.ds(pl.multiple_of((2 * core + n // 2) * 128, 128), 128)

    def fin_local(n, side):
        core = 1 - k if side else k
        return pltpu.make_async_copy(
            FIN.at[n, side], (dk_out if n % 2 else dv_out).at[:, narrow(n, core)], fl_sem.at[n, side]
        )

    def finish(n):
        remote(SND.at[n, 0, 0], RCV.at[n, 0, k], rs_sem.at[n, 0, 0], rr_sem.at[n, 0, k], sib).wait_recv()
        FIN[n, 0] = jnp.transpose(OWN[n, k] + RCV[n, 0, k].astype(F32)).astype(BF16)
        fin_local(n, 0).start()
        remote(SND.at[n, 0, 0], RCV.at[n, 0, 1 - k], rs_sem.at[n, 0, 0], rr_sem.at[n, 0, 1 - k], sib).wait_recv()
        send_sib(n).wait_recv()
        FIN[n, 1] = jnp.transpose(SIB[n, 1].astype(F32) + RCV[n, 0, 1 - k].astype(F32)).astype(BF16)
        fin_local(n, 1).start()

    complete(1)
    weigh(0, 0)
    relay(3)
    weigh(0, 1)
    partials(0)
    relay(4)
    complete(2)
    attend(0, 0)
    attend(0, 1)
    partials(1)
    query_grads(0, 0)
    query_grads(0, 1)
    complete(3)
    weigh(1, 0)
    fold(0)
    weigh(1, 1)
    partials(2)
    complete(4)
    attend(1, 0)
    attend(1, 1)
    fold(1)
    partials(3)
    split(0)
    fold(2)
    query_grads(1, 0)
    query_grads(1, 1)
    finish(0)
    split(1)
    split(2)
    split(3)
    finish(1)
    finish(2)
    finish(3)

    for n in range(4):
        send_sib(n).wait_send()
        for part in range(2):
            fin_local(n, part).wait()
            for pos in range(4):
                send_part(n, pos, part, sib).wait_send()
    for n, arr in enumerate((o_out, dq_out)):
        for h in range(2):
            out_local(n, arr, h, k).wait()
            out_remote(n, arr, h, 1 - k, k).wait_send()
            out_remote(n, arr, h, 1 - k, 1 - k).wait_recv()
    for copy in q_send:
        copy.wait_send()
    for m in msgs:
        sib_send(m).wait_send()
        for pos in range(4):
            for part in range(2):
                edge(m, pos, pos, sib, part).wait_send()


def put_out(*refs):
    copies = [pltpu.make_async_copy(refs[i], refs[4 + i], refs[8].at[i]) for i in range(4)]
    for copy in copies:
        copy.start()
    for copy in copies:
        copy.wait()


def solution(mesh):
    rows_dp = mesh.shape["dp"]

    def local(queries, key_states, value_states, grad_out, doc_ids):
        hbm, place = pl.BlockSpec(memory_space=pltpu.HBM), pl.BlockSpec(memory_space=pl.ANY)
        dma, vmem = pltpu.SemaphoreType.DMA, pltpu.VMEM
        shapes = tuple(jax.ShapeDtypeStruct((128, width), BF16) for width in (2048, 2048, 512, 512))
        made = pl.pallas_call(
            functools.partial(kernel, rows_dp),
            out_shape=shapes,
            in_specs=[hbm] * 5,
            out_specs=(place,) * 4,
            scratch_shapes=[
                vmem((2, 128, 1024), BF16),
                vmem((2, 128, 1024), BF16),
                vmem((2, 1280, 128), BF16),
                vmem((2, 1280, 128), BF16),
                vmem((5, 2, 1, 128), jnp.int32),
                vmem((2, 128, 1024), F32),
                vmem((2, 512, 1024), F32),
                vmem((2, 512, 1280), BF16),
                vmem((2, 512, 1280), BF16),
                vmem((2, 2, 2, 128, 512), BF16),
                vmem((4, 5, 128, 256), F32),
                vmem((4, 4, 2, 128, 128), BF16),
                vmem((4, 4, 2, 128, 128), BF16),
                vmem((4, 2, 128, 128), F32),
                vmem((4, 2, 128, 128), BF16),
                vmem((4, 2, 128, 128), BF16),
                dma((5,)),
                dma((5, 5, 2)),
                dma((5, 5, 2)),
                dma((2,)),
                dma((2,)),
                dma((2,)),
                dma((4, 4, 2)),
                dma((4, 4, 2)),
                dma((2, 2)),
                dma((2, 2)),
                dma((2, 2)),
                dma((4, 2)),
                dma((4,)),
                dma((4,)),
            ],
            compiler_params=pltpu.CompilerParams(
                collective_id=0, has_side_effects=True, vmem_limit_bytes=48 * 1024 * 1024
            ),
        )(*[pltpu.with_memory_space_constraint(z, pltpu.HBM) for z in (queries, key_states, value_states, grad_out, doc_ids.reshape(1, 128))])
        return pl.pallas_call(
            put_out,
            out_shape=shapes,
            in_specs=[place] * 4,
            out_specs=(hbm,) * 4,
            scratch_shapes=[dma((4,))],
            compiler_params=pltpu.CompilerParams(vmem_limit_bytes=1024 * 1024),
        )(*made)

    row, flat = P(("dp", "group"), None), P(("dp", "group"))
    return jax.shard_map(
        local,
        mesh=mesh,
        in_specs=(row, row, row, row, flat),
        out_specs=(row,) * 4,
        check_vma=False,
    )
```
